256 devices in a mesh: row: 8 (over x, core), col: 32 (over z, y).
Axes of the slice: x: 4, y: 4, z: 8, core: 2. Of those that a mesh axis runs over, the one named last changes fastest.
Arguments:
- layer_input: bfloat16 [16896, 1024], P('col', 'row'), may hold values from -6 to 6
- w_q: bfloat16 [1024, 1024], P('col', 'row'), may hold values from -0.1875 to 0.1875
- w_k: bfloat16 [1024, 1024], P('col', 'row'), may hold values from -0.1875 to 0.1875
- w_v: bfloat16 [1024, 1024], P('col', 'row'), may hold values from -0.1875 to 0.1875
- w_o: bfloat16 [1024, 1024], P('row', 'col'), may hold values from -0.375 to 0.375
- w_gate: bfloat16 [1024, 4096], P('col', 'row'), may hold values from -0.1875 to 0.1875
- w_up: bfloat16 [1024, 4096], P('col', 'row'), may hold values from -0.1875 to 0.1875
- w_down: bfloat16 [4096, 1024], P('row', 'col'), may hold values from -0.1875 to 0.1875
- norm1: float32 [1024], replicated, may hold values from 0.5 to 1.5
- norm2: float32 [1024], replicated, may hold values from 0.5 to 1.5
- q_gain: float32 [1024], P('row'), may hold values from 0.5 to 1.5
- k_gain: float32 [1024], P('row'), may hold values from 0.5 to 1.5
- bias_same: float32 [16], P('row'), may hold values from -3 to 3
- bias_diff: float32 [16], P('row'), may hold values from -3 to 3
- pre_variate: int32 [32, 512], P('col'), may hold values from 0 to 7, never falling along the last dimension, each value on 1 to 128 neighbouring positions
- pre_keep: int32 [32, 512], P('col'), may hold values 0 or 1
- dec_variate: int32 [512], P('col'), may hold values from 0 to 7
- dec_len: int32 [512], P('col'), may hold values from 1 to 1023, as said below
- dec_table: int32 [512, 8], P('col'), may hold values from 0 to 31
- dec_holder: int32 [512, 1], P('col'), may hold values from 0 to 31; in each aligned block of 16 rows (0 to 15, 16 to 31, ...) at most 2 rows name the same one
- kv_pool: bfloat16 [1024, 2, 128, 1024], P('col', None, None, 'row'), may hold values from -4 to 4
- page_variates: int32 [1024, 128], P('col'), may hold values from 0 to 7
Outputs:
- hidden: bfloat16 [16896, 1024], P('col', 'row')
- prefill_pages: bfloat16 [128, 2, 128, 1024], P('col', None, None, 'row')
- tail_pages: bfloat16 [512, 2, 128, 1024], P('col', None, None, 'row')
The draws below stay inside these ranges and needn't reach their ends.
Inputs may be any that keep to these rules, and one draw needn't show every extreme that they name: `pre_variate`: each variate's tokens form one run of at most 128 positions. `dec_len`: some request has exactly 1023 cached tokens. `dec_table`: entries past a request's last page are unused; requests may share pages. `dec_holder`: among the 16 requests of one column group at most 2 name the same holder, a bound that some block reaches of them.
All inputs are finite; a program needn't handle non-finite values. No bound on the sum of `pre_keep` on one device may be relied on, other than what follows from the above.
Results may differ from the reference program's by a relative error of at most 0.015.
Values may be sent and summed in bfloat16 or wider, within the bound.
No kernel may reach another device: no remote copies, remote signals or barrier semaphores. Data moves between devices by JAX's collectives and lax.ppermute only.
A program may use at most 128 MiB of HBM per device.

```python
import math
import jax
import jax.numpy as jnp
import numpy as np
from jax import lax

D = 1024
H = 16
HD = 64
FF = 4096
PRE = 512
DEC = 16
PG = 128
MAXP = 8
POOL_DEV = 32
VARS = 8
TOKENS = 16896
DEC_ALL = 512
CAP = 2
POOL = 1024
MAXLEN = 1024
N_ROW = 8
N_COL = 32


def draw_dec_len(key, part):
    first_key, second_key = jax.random.split(key)
    lengths = jax.random.randint(first_key, (DEC_ALL,), 1, MAXLEN)
    longest = jax.random.randint(second_key, (), 0, DEC_ALL)
    return jnp.where(jnp.arange(DEC_ALL) == longest, MAXLEN - 1, lengths).astype(jnp.int32)


def set_ends(result, rng, low, largest):
    place = [jax.random.randint(jax.random.fold_in(rng, axis), (), 0, length) for axis, length in enumerate(result.shape)]
    main_axis = result.shape.index(max(result.shape))
    next_to = place[:main_axis] + [(place[main_axis] + 1) % result.shape[main_axis]] + place[main_axis + 1:]
    return result.at[tuple(place)].set(low).at[tuple(next_to)].set(largest)


def spiked(entries, key, source, target, parts, factor):
    def block_of(axis_at):
        return (jnp.arange(entries.shape[axis_at]) // (entries.shape[axis_at] // parts)).reshape((-1,) + (1,) * (entries.ndim - 1 - axis_at))

    first = jax.random.permutation(key, parts)[block_of(target)]
    far = (block_of(target) + parts // 2) % parts
    return jnp.where((block_of(source) == first) | (block_of(source) == far), factor * entries, entries)


def shard_levels(key, shape, cuts, least, top_value):
    def one(dim, parts):
        steps = jax.random.uniform(jax.random.fold_in(jax.random.fold_in(key, 6), dim), (parts,), jnp.float32, least / len(cuts), top_value / len(cuts))
        return jnp.repeat(jnp.exp(steps), shape[dim] // parts).reshape((-1,) + (1,) * (len(shape) - dim - 1))

    level = one(*cuts[0])
    for cut in cuts[1:]:
        level = level * one(*cut)
    return level


def length_profile(number_of, total, limit, slope):
    weights = [(1 << 20) // math.isqrt(standing ** slope) + 1 for standing in range(2, number_of + 1)]
    surplus, holding = total - limit - (number_of - 1), [1] * (number_of - 1)
    while surplus > 0:
        candidates = [i for i in range(number_of - 1) if holding[i] < limit]
        pool, remaining = sum([weights[i] for i in candidates]), surplus
        for i in candidates:
            addition = min(limit - holding[i], max(1, remaining * weights[i] // pool), surplus)
            holding[i] = holding[i] + addition
            surplus = surplus - addition
    return np.array([limit] + holding)


def uneven(stream_key, amount, total, reach, lean):
    if amount == 2:
        one = jax.random.randint(stream_key, (), max(1, total - reach), min(reach, total - 1) + 1)
        return jnp.stack([one, total - one])
    sizes = jnp.asarray(length_profile(amount, total, reach, lean), jnp.int32)
    pairs = (amount - 1) // 2
    source_of, receiver = sizes[1:1 + 2 * pairs:2], sizes[2:2 + 2 * pairs:2]
    slack = jnp.minimum(source_of - 1, reach - receiver)
    shifted = jax.random.randint(jax.random.fold_in(stream_key, 1), (pairs,), 0, 1 << 20) % (slack + 1)
    sizes = sizes.at[1:1 + 2 * pairs:2].set(source_of - shifted).at[2:2 + 2 * pairs:2].set(receiver + shifted)
    return sizes[jax.random.permutation(jax.random.fold_in(stream_key, 2), amount)]


def routed_block(stream_key, own, number, rows, number_of, top, bound, skew):
    sequence = jax.random.permutation(stream_key, number_of)
    packed, usual = portions_of(number_of, rows * top, bound, skew, True), portions_of(number_of, rows * top, bound, skew, False)
    places = jnp.arange(number_of)

    def named(tallies, offset_by):
        used = int((tallies > 0).sum())
        fixed = max(1, used // 4)
        moved = fixed + (places - fixed + offset_by * (used - fixed)) % max(1, number_of - fixed)
        return jnp.zeros((number_of,), jnp.int32).at[sequence[jnp.where(places < fixed, places, moved)]].set(jnp.asarray(tallies, jnp.int32))

    tallies = jnp.where(number % 4 == 0, named(packed, number // 4), named(usual, number - number // 4 - 1))
    mixed = jax.random.permutation(jax.random.fold_in(own, 3), number_of)
    source_of, receiver = mixed[0:number_of // 2 * 2:2], mixed[1:number_of // 2 * 2:2]
    slack = jnp.minimum(tallies[source_of] - 1, bound - tallies[receiver]) // 2
    slack = jnp.where((source_of == sequence[0]) | (receiver == sequence[0]) | (tallies[receiver] == 0), 0, jnp.maximum(slack, 0))
    moved = jax.random.randint(jax.random.fold_in(own, 4), (number_of // 2,), 0, 1 << 20) % (slack + 1)
    tallies = tallies.at[source_of].add(-moved).at[receiver].add(moved)
    items = jnp.searchsorted(jnp.cumsum(tallies), jnp.arange(rows * top), side="right").astype(jnp.int32)
    listing = items.reshape(top, rows).T
    listing = listing[jax.random.permutation(jax.random.fold_in(own, 1), rows)]
    offset_by = jax.random.randint(jax.random.fold_in(own, 2), (rows, 1), 0, top)
    return jnp.take_along_axis(listing, (jnp.arange(top)[None, :] + offset_by) % top, axis=1)


def portions_of(amount, total, limit, slope, full):
    weights = [(1 << 20) // math.isqrt(standing ** slope) + 1 for standing in range(1, amount + 1)]
    largest = limit if full else min(limit, max(-(-total // amount), total * weights[0] // sum(weights)))
    least = 1 if total - largest >= amount - 1 else 0
    holding, spare = [largest] + [least] * (amount - 1), total - largest - least * (amount - 1)
    while spare > 0:
        candidates = [i for i in range(1, amount) if holding[i] < largest] or [i for i in range(1, amount) if holding[i] < limit]
        whole, left = sum([weights[i] for i in candidates]), spare
        for i in candidates:
            more = min(limit - holding[i], max(1, left * weights[i] // whole), spare)
            holding[i] = holding[i] + more
            spare = spare - more
    return np.array(holding)


def gaussian(own_key, extent, width, most, shards=(), held_as=jnp.bfloat16):
    result = width * jax.random.normal(own_key, extent, jnp.float32)
    if shards:
        result = result * shard_levels(own_key, extent, shards, -0.22, 0.18)
    return jnp.clip(result, -most, most).astype(held_as)


def heavy_noise(own_key, dims, deviation, bound, pieces, heavy, kind=jnp.bfloat16):
    result = deviation * jax.random.normal(own_key, dims, jnp.float32)
    if pieces:
        result = result * shard_levels(own_key, dims, pieces, -0.22, 0.18)
    return jnp.clip(spiked(result, jax.random.fold_in(own_key, 3), *heavy), -bound, bound).astype(kind)


def setup_inputs(seed: int = 0) -> dict:
    key_list = jax.random.split(jax.random.key(seed), 23)
    layer_input = gaussian(key_list[0], (TOKENS, D), 1.0, 6.0, ((0, 32), (1, 8)))
    w_q = gaussian(key_list[1], (D, D), D ** -0.5, 0.1875, ((0, 32), (1, 8)))
    w_k = gaussian(key_list[2], (D, D), D ** -0.5, 0.1875, ((0, 32), (1, 8)))
    w_v = gaussian(key_list[3], (D, D), D ** -0.5, 0.1875, ((0, 32), (1, 8)))
    w_o = heavy_noise(key_list[4], (D, D), D ** -0.5, 0.375, ((0, 8), (1, 32)), (0, 1, 32, 2.75))
    w_gate = gaussian(key_list[5], (D, FF), D ** -0.5, 0.1875, ((0, 32), (1, 8)))
    w_up = gaussian(key_list[6], (D, FF), D ** -0.5, 0.1875, ((0, 32), (1, 8)))
    w_down = heavy_noise(key_list[7], (FF, D), FF ** -0.5, 0.1875, ((0, 8), (1, 32)), (0, 1, 32, 2.75))
    norm1 = jnp.clip(1.0 + 0.1 * jax.random.normal(key_list[8], (D,), jnp.float32), 0.5, 1.5)
    norm2 = jnp.clip(1.0 + 0.1 * jax.random.normal(key_list[9], (D,), jnp.float32), 0.5, 1.5)
    q_gain = jnp.clip(1.0 + 0.1 * jax.random.normal(key_list[10], (D,), jnp.float32), 0.5, 1.5)
    k_gain = jnp.clip(1.0 + 0.1 * jax.random.normal(key_list[11], (D,), jnp.float32), 0.5, 1.5)
    bias_same = gaussian(key_list[12], (H,), 1.0, 3.0, ((0, 8),), jnp.float32)
    bias_diff = gaussian(key_list[13], (H,), 1.0, 3.0, ((0, 8),), jnp.float32)
    pre_variate = jax.vmap(lambda own: jnp.searchsorted(jnp.cumsum(uneven(own, VARS, PRE, 2 * PRE // VARS, 1)), jnp.arange(PRE), side="right"))(jax.random.split(key_list[14], N_COL)).reshape((N_COL, PRE)).astype(jnp.int32)
    pre_keep = set_ends((jax.random.randint(key_list[15], (N_COL, PRE), 0, 8) < 7).astype(jnp.int32), jax.random.fold_in(key_list[15], 1), 0, 1)
    dec_variate = set_ends(jax.random.randint(key_list[16], (DEC_ALL,), 0, VARS), jax.random.fold_in(key_list[16], 1), 0, VARS - 1).astype(jnp.int32)
    dec_len = draw_dec_len(jax.random.fold_in(key_list[22], 71), 0)
    dec_table = set_ends(jax.random.randint(key_list[18], (DEC_ALL, MAXP), 0, POOL_DEV), jax.random.fold_in(key_list[18], 1), 0, POOL_DEV - 1).astype(jnp.int32)
    dec_holder_keys = jax.random.split(jax.random.fold_in(key_list[19], 1), DEC_ALL // DEC)
    dec_holder_turns = jax.random.permutation(jax.random.fold_in(key_list[19], 3), DEC_ALL // DEC)
    dec_holder = jax.vmap(lambda own, number: routed_block(jax.random.fold_in(key_list[19], 2), own, number, DEC, N_COL, 1, CAP, 2))(dec_holder_keys, dec_holder_turns).reshape((DEC_ALL, 1))
    kv_pool = gaussian(key_list[20], (POOL, 2, PG, D), 1.0, 4.0, ((0, 32), (3, 8)))
    page_variates = set_ends(jax.random.randint(key_list[21], (POOL, PG), 0, VARS), jax.random.fold_in(key_list[21], 1), 0, VARS - 1).astype(jnp.int32)
    return {"layer_input": layer_input, "w_q": w_q, "w_k": w_k, "w_v": w_v, "w_o": w_o, "w_gate": w_gate, "w_up": w_up, "w_down": w_down, "norm1": norm1, "norm2": norm2, "q_gain": q_gain, "k_gain": k_gain, "bias_same": bias_same, "bias_diff": bias_diff, "pre_variate": pre_variate, "pre_keep": pre_keep, "dec_variate": dec_variate, "dec_len": dec_len, "dec_table": dec_table, "dec_holder": dec_holder, "kv_pool": kv_pool, "page_variates": page_variates}


eps = 1e-05

def norm_rows(values, gain_row):
    return values * lax.rsqrt(lax.optimization_barrier(jnp.mean(values * values, axis=-1, keepdims=True)) + eps) * gain_row

def rotate(tensor, places):
    half_size = tensor.shape[-1] // 2
    spacing = jnp.arange(half_size).astype(jnp.float32) * (2.0 / tensor.shape[-1])
    angles = places.astype(jnp.float32)[:, None] * jnp.power(10000.0, -spacing)[None, :]
    cosine = jnp.cos(angles)[:, None, :]
    sine_part = jnp.sin(angles)[:, None, :]
    lower_half = tensor[..., :half_size]
    upper_half = tensor[..., half_size:]
    return jnp.concatenate([lower_half * cosine - upper_half * sine_part, upper_half * cosine + lower_half * sine_part], axis=-1)

def segment_time(variates):
    places = jnp.arange(variates.shape[0]).astype(jnp.int32)
    run_start = jnp.concatenate([jnp.ones((1,), dtype=jnp.bool_), variates[1:] != variates[:-1]])
    starts = lax.cummax(jnp.where(run_start, places, 0).astype(jnp.int32), axis=0)
    return places - starts

def row_sum(left_rows, weight, groups):
    width_each = left_rows.shape[1] // groups
    summed = jnp.zeros((left_rows.shape[0], weight.shape[1]), jnp.float32)
    for group_index in range(groups):
        lo_col = group_index * width_each
        partial_value = jnp.dot(left_rows[:, lo_col:lo_col + width_each], weight[lo_col:lo_col + width_each], preferred_element_type=jnp.float32)
        rounded = lax.optimization_barrier(partial_value.astype(jnp.bfloat16))
        summed = summed + rounded.astype(jnp.float32)
    return summed

def reference(layer_input, w_q, w_k, w_v, w_o, w_gate, w_up, w_down, norm1, norm2, q_gain, k_gain, bias_same, bias_diff, pre_variate, pre_keep, dec_variate, dec_len, dec_table, dec_holder, kv_pool, page_variates):
    score_scale = HD ** (-0.5)
    resid_in = layer_input.astype(jnp.float32)
    normed = norm_rows(resid_in, norm1).astype(jnp.bfloat16)
    query_proj = jnp.dot(normed, w_q, preferred_element_type=jnp.float32)
    key_proj = jnp.dot(normed, w_k, preferred_element_type=jnp.float32)
    value_proj = jnp.dot(normed, w_v, preferred_element_type=jnp.float32)
    pre_times = jax.vmap(segment_time)(pre_variate)
    places = jnp.concatenate([pre_times, dec_len.reshape(N_COL, DEC)], axis=1).reshape(-1)
    query_rot = rotate(norm_rows(query_proj.reshape(-1, H, HD), q_gain.reshape(H, HD)), places).astype(jnp.bfloat16)
    key_rot = rotate(norm_rows(key_proj.reshape(-1, H, HD), k_gain.reshape(H, HD)), places).astype(jnp.bfloat16)
    value_bf = value_proj.astype(jnp.bfloat16).reshape(-1, H, HD)
    grouped_q = query_rot.reshape(N_COL, PRE + DEC, H, HD)
    grouped_k = key_rot.reshape(N_COL, PRE + DEC, H, HD)
    grouped_v = value_bf.reshape(N_COL, PRE + DEC, H, HD)

    def prefill_group(inputs):
        pre_queries, pre_keys, pre_values, variates, keep_mask = inputs
        scores = jnp.einsum('qhd,khd->hqk', pre_queries.astype(jnp.float32), pre_keys.astype(jnp.float32)) * score_scale
        same_var = variates[:, None] == variates[None, :]
        scores = scores + jnp.where(same_var[None], bias_same[:, None, None], bias_diff[:, None, None])
        allowed = (keep_mask[None, :] == 1) | (jnp.arange(PRE)[:, None] == jnp.arange(PRE)[None, :])
        exp_scores = jnp.where(allowed[None], jnp.exp(scores), 0.0)
        weights_bf = (exp_scores / lax.optimization_barrier(jnp.sum(exp_scores, axis=2, keepdims=True))).astype(jnp.bfloat16)
        return jnp.einsum('hqk,khd->qhd', weights_bf.astype(jnp.float32), pre_values.astype(jnp.float32)).astype(jnp.bfloat16)
    pre_out = lax.map(prefill_group, (grouped_q[:, :PRE], grouped_k[:, :PRE], grouped_v[:, :PRE], pre_variate, pre_keep))

    def decode_one(inputs):
        new_query, new_key, new_value, page_rows, length, variate, holder = inputs
        pool_rows = holder * POOL_DEV + page_rows
        gathered = kv_pool[pool_rows]
        cached_keys = gathered[:, 0].reshape(MAXP * PG, H, HD)
        cached_vals = gathered[:, 1].reshape(MAXP * PG, H, HD)
        key_variates = page_variates[pool_rows].reshape(MAXP * PG)
        scores = jnp.einsum('hd,khd->hk', new_query.astype(jnp.float32), cached_keys.astype(jnp.float32)) * score_scale
        scores = scores + jnp.where((key_variates == variate)[None, :], bias_same[:, None], bias_diff[:, None])
        own_score = lax.optimization_barrier(jnp.sum(new_query.astype(jnp.float32) * new_key.astype(jnp.float32), axis=1)) * score_scale + bias_same
        exp_scores = jnp.where((jnp.arange(MAXP * PG) < length)[None, :], jnp.exp(scores), 0.0)
        own_exp = jnp.exp(own_score)
        total_weight = lax.optimization_barrier(jnp.sum(exp_scores, axis=1)) + own_exp
        weights_bf = (exp_scores / total_weight[:, None]).astype(jnp.bfloat16)
        own_weight = (own_exp / total_weight).astype(jnp.bfloat16)
        attended = jnp.einsum('hk,khd->hd', weights_bf.astype(jnp.float32), cached_vals.astype(jnp.float32)) + own_weight.astype(jnp.float32)[:, None] * new_value.astype(jnp.float32)
        tail_slot = pool_rows[length // PG]
        old_page = kv_pool[tail_slot]
        hit_row = (jnp.arange(PG) == length % PG)[None, :, None]
        new_rows = jnp.stack([new_key.reshape(D), new_value.reshape(D)])[:, None, :]
        return (attended.astype(jnp.bfloat16), jnp.where(hit_row, new_rows, old_page))
    dec_queries = grouped_q[:, PRE:].reshape(N_COL * DEC, H, HD)
    dec_keys = grouped_k[:, PRE:].reshape(N_COL * DEC, H, HD)
    dec_values = grouped_v[:, PRE:].reshape(N_COL * DEC, H, HD)
    dec_out, tail_pages = lax.map(decode_one, (dec_queries, dec_keys, dec_values, dec_table, dec_len, dec_variate, dec_holder[:, 0]))
    all_attended = jnp.concatenate([pre_out.reshape(N_COL, PRE, D), dec_out.reshape(N_COL, DEC, D)], axis=1).reshape(-1, D)
    attn_total = row_sum(all_attended, w_o, N_ROW)
    resid_full = resid_in + attn_total
    ffn_input = norm_rows(resid_full, norm2).astype(jnp.bfloat16)
    gate_proj = jnp.dot(ffn_input, w_gate, preferred_element_type=jnp.float32)
    up_proj = jnp.dot(ffn_input, w_up, preferred_element_type=jnp.float32)
    hidden_units = (jax.nn.silu(gate_proj) * up_proj).astype(jnp.bfloat16)
    ffn_total = row_sum(hidden_units, w_down, N_ROW)
    hidden = (resid_full + ffn_total).astype(jnp.bfloat16)
    prefill_pages = jnp.stack([grouped_k[:, :PRE].reshape(-1, PG, D), grouped_v[:, :PRE].reshape(-1, PG, D)], axis=1)
    return (hidden, prefill_pages, tail_pages)
```

```python
import functools

import jax
import jax.numpy as jnp
import numpy as np
from jax import lax
from jax.experimental import pallas as pl
from jax.experimental.pallas import tpu as pltpu
from jax.sharding import PartitionSpec as P

HD = 64
EPS = 1e-05
BF = jnp.bfloat16
F32 = jnp.float32


def dot_nt(a, b):
    return lax.dot_general(a, b, (((1,), (1,)), ((), ())), preferred_element_type=F32)


def whole(shape):
    zeros = (0,) * len(shape)
    return pl.BlockSpec(shape, lambda *_: zeros)


def in_order(me_ref, same_ref, other_ref):
    x, core = me_ref[0], me_ref[1]
    chips = same_ref.shape[0]
    parts = []
    for j in range(2 * chips):
        away = lax.rem(x - j // 2 + chips, chips)
        parts.append(jnp.where(core == j % 2, same_ref[away].astype(F32), other_ref[away].astype(F32)))
    return jnp.concatenate(parts, axis=1)


def norm_rotate(t, gain, cos, sin):
    lane = lax.broadcasted_iota(jnp.int32, t.shape, 1)
    first_head = lane < HD
    lower = (lane % HD) < (HD // 2)
    sq = t * t
    s0 = jnp.sum(jnp.where(first_head, sq, 0.0), axis=-1, keepdims=True)
    s1 = jnp.sum(jnp.where(first_head, 0.0, sq), axis=-1, keepdims=True)
    r = jnp.where(first_head, lax.rsqrt(s0 * (1.0 / HD) + EPS), lax.rsqrt(s1 * (1.0 / HD) + EPS))
    t = t * r * gain
    partner = jnp.where(
        lower, pltpu.roll(t, 128 - HD // 2, axis=1), pltpu.roll(t, HD // 2, axis=1)
    )
    return t * cos + partner * sin


def norm_features(x, gain):
    scale = lax.rsqrt(jnp.mean(x * x, axis=-1, keepdims=True) + EPS)
    return (x * scale * gain).astype(BF)


def pack_kernel(table_ref, len_ref, var_ref, holder_ref, x_ref, w_ref, out_ref):
    peers = out_ref.shape[0]
    share = w_ref.shape[0]
    count, entries = table_ref.shape
    w = w_ref[...]
    for c in range(peers):
        out_ref[c, 0:share, :] = w
        out_ref[c, share : share + 8, :] = jnp.zeros((8, 128), BF)
    lane = lax.broadcasted_iota(jnp.int32, (8, 128), 1)
    sub = lax.broadcasted_iota(jnp.int32, (8, 128), 0)
    for r in range(count):
        holder = holder_ref[r, 0]
        rank = jnp.int32(0)
        for p in range(r):
            rank = rank + (holder_ref[p, 0] == holder).astype(jnp.int32)
        length = len_ref[r]
        facts = [table_ref[r, p] for p in range(entries)]
        facts += [length // 128, length % 128, var_ref[r]]
        vec = jnp.zeros((8, 128), jnp.int32)
        for j, fact in enumerate(facts):
            vec = jnp.where(lane == j, fact, vec)
        x = jnp.broadcast_to(x_ref[r : r + 1, :].astype(F32), (8, 128))
        old = out_ref[holder, share : share + 8, :].astype(F32)
        new = jnp.where(sub == rank, vec.astype(F32), jnp.where(sub == rank + 2, x, old))
        out_ref[holder, share : share + 8, :] = new.astype(BF)


def pack_call(table, length, variate, holder, x, w, peers):
    count = length.shape[0]
    smem = pl.BlockSpec(memory_space=pltpu.SMEM)
    shape = (peers, w.shape[0] + 8, 128)
    last = x.shape[0] // count - 1
    return pl.pallas_call(
        pack_kernel,
        grid=(1,),
        in_specs=[
            smem,
            smem,
            smem,
            smem,
            pl.BlockSpec((count, 128), lambda i: (last, 0)),
            whole(w.shape),
        ],
        out_specs=whole(shape),
        out_shape=jax.ShapeDtypeStruct(shape, BF),
        cost_estimate=pl.CostEstimate(flops=0, bytes_accessed=1024 * 1024, transcendentals=0),
        name="pack",
    )(table, length, variate, holder, x, w)


def qkv_kernel(
    me_ref, xa_ref, xb_ref, norm_ref, wq_ref, wk_ref, wv_ref, cos_ref, sin_ref, qg_ref, kg_ref, out_ref
):
    normed = norm_features(in_order(me_ref, xa_ref, xb_ref), norm_ref[...])
    share = wq_ref.shape[1] - 8
    wq = wq_ref[:, 0:share, :].reshape(-1, 128)
    w = jnp.concatenate([wq, wk_ref[...], wv_ref[...]], axis=1)
    proj = jnp.dot(normed, w, preferred_element_type=F32)
    cos = cos_ref[...]
    sin = sin_ref[...]
    out_ref[:, 0:128] = norm_rotate(proj[:, 0:128], qg_ref[...], cos, sin).astype(BF)
    out_ref[:, 128:256] = norm_rotate(proj[:, 128:256], kg_ref[...], cos, sin).astype(BF)
    out_ref[:, 256:384] = proj[:, 256:384].astype(BF)


def qkv_call(me, xa, xb, norm1, got, big, col_block, cos, sin, qg, kg):
    chips, rows, _ = xa.shape
    width = norm1.shape[1]
    step = rows // 3
    row_spec = lambda cols: pl.BlockSpec((step, cols), lambda i: (i, 0))
    x_spec = pl.BlockSpec((chips, step, 128), lambda i: (0, i, 0))
    return pl.pallas_call(
        qkv_kernel,
        grid=(3,),
        in_specs=[
            pl.BlockSpec(memory_space=pltpu.SMEM),
            x_spec,
            x_spec,
            whole((1, width)),
            whole(got.shape),
            pl.BlockSpec((width, 128), lambda i: (0, col_block)),
            pl.BlockSpec((width, 128), lambda i: (0, col_block + 1)),
            row_spec(128),
            row_spec(128),
            whole((1, 128)),
            whole((1, 128)),
        ],
        out_specs=row_spec(384),
        out_shape=jax.ShapeDtypeStruct((rows, 384), BF),
        cost_estimate=pl.CostEstimate(
            flops=2 * rows * width * 384, bytes_accessed=4 * 1024 * 1024, transcendentals=0
        ),
        name="qkv",
    )(me, xa, xb, norm1, got, big, big, cos, sin, qg, kg)


def prefill_kernel(
    qkv_ref, vcol_ref, vrow_ref, keep_ref, bsame_ref, bdiff_ref, out_ref, pages_ref
):
    length = out_ref.shape[0]
    block = 128
    keys = qkv_ref[0:length, 128:256]
    values = qkv_ref[0:length, 256:384]
    for p in range(length // 128):
        pages_ref[p, 0] = qkv_ref[p * 128 : (p + 1) * 128, 128:256]
        pages_ref[p, 1] = qkv_ref[p * 128 : (p + 1) * 128, 256:384]
    lane = lax.broadcasted_iota(jnp.int32, (block, 128), 1)
    first_head = lane < HD
    col = lax.broadcasted_iota(jnp.int32, (block, length), 1)
    row = lax.broadcasted_iota(jnp.int32, (block, length), 0)
    keep = keep_ref[...] == 1
    for b in range(length // block):
        q = qkv_ref[b * block : (b + 1) * block, 0:128]
        same = vcol_ref[b * block : (b + 1) * block, :] == vrow_ref[...]
        allowed = keep | (col == row + b * block)
        outs = []
        for h in range(2):
            qh = jnp.where(first_head if h == 0 else ~first_head, q, jnp.zeros_like(q))
            s = dot_nt(qh, keys) * (HD**-0.5)
            s = s + jnp.where(same, bsame_ref[h], bdiff_ref[h])
            e = jnp.where(allowed, jnp.exp(s), 0.0)
            total = jnp.sum(e, axis=1, keepdims=True)
            w = (e * (1.0 / total)).astype(BF)
            outs.append(jnp.dot(w, values, preferred_element_type=F32))
        out_ref[b * block : (b + 1) * block, :] = jnp.where(first_head, outs[0], outs[1]).astype(BF)


def prefill_call(qkv, vcol, vrow, keep, bsame, bdiff, length, page):
    smem = pl.BlockSpec(memory_space=pltpu.SMEM)
    return pl.pallas_call(
        prefill_kernel,
        grid=(1,),
        in_specs=[
            whole(qkv.shape),
            whole((length, 1)),
            whole((1, length)),
            whole((1, length)),
            smem,
            smem,
        ],
        out_specs=[whole((length, 128)), whole((length // page, 2, page, 128))],
        out_shape=[
            jax.ShapeDtypeStruct((length, 128), BF),
            jax.ShapeDtypeStruct((length // page, 2, page, 128), BF),
        ],
        cost_estimate=pl.CostEstimate(
            flops=8 * length * length * 128,
            bytes_accessed=8 * length * 128 * 2,
            transcendentals=2 * length * length,
        ),
        name="prefill",
    )(qkv, vcol, vrow, keep, bsame, bdiff)


def decode_kernel(
    me_ref,
    xa_ref,
    xb_ref,
    norm_ref,
    w_ref,
    cos_ref,
    sin_ref,
    qg_ref,
    ints_ref,
    bsame_ref,
    bdiff_ref,
    pool_ref,
    pv_ref,
    out_ref,
):
    slots = ints_ref.shape[0]
    pages = pool_ref.shape[0]
    lane = lax.broadcasted_iota(jnp.int32, (slots, 128), 1)
    first_head = lane < HD
    normed = norm_features(in_order(me_ref, xa_ref, xb_ref), norm_ref[...])
    wq = w_ref[:, 0 : w_ref.shape[1] - 8, :].reshape(-1, 128)
    q = jnp.dot(normed, wq, preferred_element_type=F32)
    q = norm_rotate(q, qg_ref[...], cos_ref[...], sin_ref[...]).astype(BF)
    zero = jnp.zeros_like(q)
    q2 = jnp.concatenate([jnp.where(first_head, q, zero), jnp.where(first_head, zero, q)], axis=0)
    rows = lax.broadcasted_iota(jnp.int32, (2 * slots, 1), 0)
    bsame = jnp.where(rows < slots, bsame_ref[0], bsame_ref[1])
    bdiff = jnp.where(rows < slots, bdiff_ref[0], bdiff_ref[1])
    ints = jnp.concatenate([ints_ref[...], ints_ref[...]], axis=0)
    entries = ints.shape[1] // 2
    last = ints[:, entries : entries + 1]
    rem = ints[:, entries + 1 : entries + 2]
    var = ints[:, entries + 2 : entries + 3]
    tok = lax.broadcasted_iota(jnp.int32, (2 * slots, 128), 1)
    in_part = (tok < rem).astype(F32)
    full = jnp.zeros((2 * slots, 128), F32)
    part = jnp.zeros((2 * slots, 128), F32)
    for p in range(entries):
        hit = (ints[:, p : p + 1] == tok).astype(F32)
        full = full + jnp.where(p < last, hit, 0.0)
        part = part + jnp.where(p == last, hit, 0.0)
    acc = jnp.zeros((2 * slots, 128), F32)
    sums = jnp.zeros((2 * slots, 128), F32)
    for g in range(pages):
        s = dot_nt(q2, pool_ref[g, 0]) * (HD**-0.5)
        s = s + jnp.where(pv_ref[g : g + 1, :] == var, bsame, bdiff)
        count = full[:, g : g + 1] + part[:, g : g + 1] * in_part
        e = jnp.exp(s) * count
        sums = sums + e
        acc = acc + jnp.dot(e.astype(BF), pool_ref[g, 1], preferred_element_type=F32)
    total = jnp.sum(sums, axis=1, keepdims=True)
    o = acc / jnp.where(total > 0.0, total, 1.0)
    out_ref[:, 0:128] = jnp.where(first_head, o[0:slots], o[slots:]).astype(BF)
    high = total.astype(BF).astype(F32)
    low = total - high
    out_ref[:, 128:256] = jnp.where(
        lane < 2,
        jnp.where(lane == 0, high[0:slots], high[slots:]),
        jnp.where(lane == 2, low[0:slots], low[slots:]),
    ).astype(BF)


def decode_call(me, xa, xb, norm1, got, cos, sin, qg, ints, bsame, bdiff, pool, pv):
    slots = ints.shape[0]
    smem = pl.BlockSpec(memory_space=pltpu.SMEM)
    args = (me, xa, xb, norm1, got, cos, sin, qg, ints, bsame, bdiff, pool, pv)
    return pl.pallas_call(
        decode_kernel,
        grid=(1,),
        in_specs=[smem if i in (0, 9, 10) else whole(a.shape) for i, a in enumerate(args)],
        out_specs=whole((slots, 256)),
        out_shape=jax.ShapeDtypeStruct((slots, 256), BF),
        cost_estimate=pl.CostEstimate(
            flops=4 * 128 * 128 * 4096, bytes_accessed=3 * 1024 * 1024, transcendentals=128 * 4096
        ),
        name="decode",
    )(*args)


def out_proj_kernel(
    me_ref, bsame_ref, pre_ref, new_ref, back_ref, pick_ref, w_ref, own_ref, other_ref
):
    x, core = me_ref[0], me_ref[1]
    length = pre_ref.shape[0]
    chips = own_ref.shape[0]
    pre = pre_ref[...]
    first_head = lax.broadcasted_iota(jnp.int32, (new_ref.shape[0], 128), 1) < HD
    got = jnp.dot(pick_ref[...], back_ref[...], preferred_element_type=F32)
    total = jnp.where(
        first_head, got[:, 128:129] + got[:, 130:131], got[:, 129:130] + got[:, 131:132]
    )
    qk = new_ref[:, 0:128].astype(F32) * new_ref[:, 128:256].astype(F32)
    s0 = jnp.sum(jnp.where(first_head, qk, 0.0), axis=1, keepdims=True)
    s1 = jnp.sum(jnp.where(first_head, 0.0, qk), axis=1, keepdims=True)
    own = jnp.where(
        first_head,
        jnp.exp(s0 * (HD**-0.5) + bsame_ref[0]),
        jnp.exp(s1 * (HD**-0.5) + bsame_ref[1]),
    )
    value = new_ref[:, 256:384].astype(F32)
    dec = ((got[:, 0:128] * total + own * value) / (total + own)).astype(BF)
    for away in range(chips):
        chip = lax.rem(x + away, chips)
        w = w_ref[pl.ds(pl.multiple_of(chip * 256, 256), 256), :]
        for left, start, size in ((pre, 0, length), (dec, length, dec.shape[0])):
            o = dot_nt(left, w).astype(BF)
            own_ref[away, start : start + size, :] = jnp.where(core == 0, o[:, :128], o[:, 128:])
            other_ref[away, start : start + size, :] = jnp.where(core == 0, o[:, 128:], o[:, :128])


def out_proj_call(me, bsame, pre, qkv, back, pick, big, col_block):
    length = pre.shape[0]
    rows = length + pick.shape[0]
    width = big.shape[0]
    chips = width // 256
    half = jax.ShapeDtypeStruct((chips, rows, 128), BF)
    return pl.pallas_call(
        out_proj_kernel,
        grid=(1,),
        in_specs=[
            pl.BlockSpec(memory_space=pltpu.SMEM),
            pl.BlockSpec(memory_space=pltpu.SMEM),
            whole(pre.shape),
            pl.BlockSpec((pick.shape[0], 384), lambda i: (length // pick.shape[0], 0)),
            whole(back.shape),
            whole(pick.shape),
            pl.BlockSpec((width, 128), lambda i: (0, col_block)),
        ],
        out_specs=[whole(half.shape), whole(half.shape)],
        out_shape=[half, half],
        cost_estimate=pl.CostEstimate(
            flops=2 * rows * 128 * width, bytes_accessed=2 * 1024 * 1024, transcendentals=0
        ),
        name="out_proj",
    )(me, bsame, pre, qkv, back, pick, big)


def ffn_kernel(me_ref, ra_ref, rb_ref, norm_ref, gate_ref, up_ref, down_ref, own_ref, other_ref):
    x, core = me_ref[0], me_ref[1]
    chips = ra_ref.shape[0]
    r = in_order(me_ref, ra_ref, rb_ref)
    scale = lax.rsqrt(jnp.mean(r * r, axis=-1, keepdims=True) + EPS)
    normed = (r * scale * norm_ref[...]).astype(BF)
    gate = jnp.dot(normed, gate_ref[...], preferred_element_type=F32)
    up = jnp.dot(normed, up_ref[...], preferred_element_type=F32)
    units = (gate * (1.0 / (1.0 + jnp.exp(-gate))) * up).astype(BF)
    for away in range(chips):
        chip = lax.rem(x + away, chips)
        w = down_ref[pl.ds(pl.multiple_of(chip * 256, 256), 256), :]
        o = dot_nt(units, w).astype(BF)
        own_ref[away] = jnp.where(core == 0, o[:, :128], o[:, 128:])
        other_ref[away] = jnp.where(core == 0, o[:, 128:], o[:, :128])


def ffn_call(me, ra, rb, norm2, big, hidden):
    chips, rows, _ = ra.shape
    width = big.shape[0]
    step = rows // 3
    w_spec = lambda b: pl.BlockSpec((width, hidden), lambda i: (0, b))
    r_spec = pl.BlockSpec((chips, step, 128), lambda i: (0, i, 0))
    half = jax.ShapeDtypeStruct((chips, rows, 128), BF)
    return pl.pallas_call(
        ffn_kernel,
        grid=(3,),
        in_specs=[
            pl.BlockSpec(memory_space=pltpu.SMEM),
            r_spec,
            r_spec,
            whole((1, width)),
            w_spec(0),
            w_spec(1),
            w_spec(2),
        ],
        out_specs=[r_spec, r_spec],
        out_shape=[half, half],
        cost_estimate=pl.CostEstimate(
            flops=6 * rows * width * hidden, bytes_accessed=6 * 1024 * 1024, transcendentals=0
        ),
        compiler_params=pltpu.CompilerParams(vmem_limit_bytes=32 * 1024 * 1024),
        name="ffn",
    )(me, ra, rb, norm2, big, big, big)


def tail_kernel(target_ref, row_ref, new_ref, pages_ref, out_ref, sem):
    count = out_ref.shape[0]
    copies = [
        pltpu.make_async_copy(pages_ref.at[target_ref[r]], out_ref.at[r], sem.at[r])
        for r in range(count)
    ]
    for c in copies:
        c.start()
    for r in range(count):
        copies[r].wait()
        row = row_ref[r]
        start = pl.multiple_of((row // 16) * 16, 16)
        hit = lax.broadcasted_iota(jnp.int32, (16, 128), 0) == row - start
        for i in range(2):
            new = new_ref[r : r + 1, (1 + i) * 128 : (2 + i) * 128].astype(F32)
            old = out_ref[r, i, pl.ds(start, 16), :].astype(F32)
            out_ref[r, i, pl.ds(start, 16), :] = jnp.where(hit, new, old).astype(BF)


def tail_call(target, row, new, pages):
    count = target.shape[0]
    smem = pl.BlockSpec(memory_space=pltpu.SMEM)
    shape = (count,) + pages.shape[1:]
    return pl.pallas_call(
        tail_kernel,
        grid=(1,),
        in_specs=[
            smem,
            smem,
            pl.BlockSpec((count, 384), lambda i: (new.shape[0] // count - 1, 0)),
            pl.BlockSpec(memory_space=pl.ANY),
        ],
        out_specs=whole(shape),
        out_shape=jax.ShapeDtypeStruct(shape, BF),
        scratch_shapes=[pltpu.SemaphoreType.DMA((count,))],
        cost_estimate=pl.CostEstimate(
            flops=0, bytes_accessed=4 * 1024 * 1024, transcendentals=0
        ),
        name="tail",
    )(target, row, new, pages)


def shifted(x, axis, size, stride, step):
    n = lax.axis_size(axis)
    span = size * stride
    pairs = []
    for i in range(n):
        place = (i % span) // stride
        pairs.append((i, i + ((place + step) % size - place) * stride))
    return lax.ppermute(x, axis, pairs)


def row_gather(v, chips):
    parts = [v] + [shifted(v, "row", chips, 2, d) for d in range(1, chips)]
    same = jnp.stack(parts)
    return same, shifted(same, "row", 2, 1, 1)


def row_scatter(own, other):
    chips = own.shape[0]
    total = own.astype(F32) + shifted(other, "row", 2, 1, 1).astype(F32)
    result = total[0]
    for d in range(1, chips):
        result = result + shifted(total[d].astype(BF), "row", chips, 2, d).astype(F32)
    return result


def exchange(x, axis):
    return lax.all_to_all(x, axis, split_axis=0, concat_axis=0, tiled=True)


def on_device(
    layer_input,
    w_q,
    w_k,
    w_v,
    w_o,
    w_gate,
    w_up,
    w_down,
    norm1,
    norm2,
    q_gain,
    k_gain,
    bias_same,
    bias_diff,
    pre_variate,
    pre_keep,
    dec_variate,
    dec_len,
    dec_table,
    dec_holder,
    kv_pool,
    page_variates,
):
    rows, width = layer_input.shape
    pre_len = pre_variate.shape[1]
    dec_count = dec_len.shape[0]
    hidden = w_gate.shape[1]
    page = kv_pool.shape[2]
    page_count = dec_table.shape[1]
    pool_pages = kv_pool.shape[0]
    peers = lax.axis_size("col")
    slots = 2
    chips = lax.axis_size("row") // 2
    row_at = lax.axis_index("row")
    me = jnp.stack([row_at // 2, row_at % 2]).astype(jnp.int32)

    sent = pack_call(dec_table, dec_len, dec_variate, dec_holder, layer_input, w_q, peers)
    got = exchange(sent, "col")
    big = lax.all_gather(
        jnp.concatenate([w_gate, w_up, w_down.T, w_o.T, w_k, w_v], axis=1),
        "col",
        axis=0,
        tiled=True,
    )
    xa, xb = row_gather(layer_input, chips)

    slot_rows = got[:, -8 : 2 * slots - 8]
    got_x = slot_rows[:, slots:].reshape(peers * slots, width)
    sa, sb = row_gather(got_x, chips)
    got_ints = slot_rows[:, :slots, : 2 * page_count].astype(jnp.int32)
    got_ints = got_ints.reshape(peers * slots, 2 * page_count)
    got_last = got_ints[:, page_count]
    entry = jnp.arange(page_count)[None, :]
    tail_slot = jnp.sum(
        jnp.where(entry == got_last[:, None], got_ints[:, :page_count], 0), axis=1
    )
    old_tails = kv_pool[tail_slot].reshape(peers, slots, 2, page, width)

    half = HD // 2
    spacing = (jnp.arange(width) % half).astype(F32) * (2.0 / HD)
    rates = jnp.power(10000.0, -spacing)[None, :]
    sign = jnp.where((jnp.arange(width) % HD) < half, -1.0, 1.0)[None, :]

    def turns(times):
        angles = times.astype(F32)[:, None] * rates
        return jnp.cos(angles), jnp.sin(angles) * sign

    cos_slots, sin_slots = turns(got_last * page + got_ints[:, page_count + 1])
    dec = decode_call(
        me,
        sa,
        sb,
        norm1[None],
        got,
        cos_slots,
        sin_slots,
        q_gain[None],
        got_ints,
        bias_same,
        bias_diff,
        kv_pool,
        page_variates,
    )
    back = exchange(dec.reshape(peers, slots, 2 * width), "col").reshape(
        peers * slots, 2 * width
    )
    old_tails, back = lax.optimization_barrier((old_tails, back))
    tails = exchange(old_tails, "col")

    holder = dec_holder[:, 0]
    earlier = jnp.arange(dec_count)[:, None] > jnp.arange(dec_count)[None, :]
    rank = jnp.sum(((holder[:, None] == holder[None, :]) & earlier).astype(jnp.int32), axis=1)
    target = holder * slots + rank
    pick = (target[:, None] == jnp.arange(peers * slots)[None, :]).astype(BF)
    variates = pre_variate[0]
    starts = jnp.sum((variates[None, :] < variates[:, None]).astype(jnp.int32), axis=1)
    cos, sin = turns(jnp.concatenate([jnp.arange(pre_len) - starts, dec_len]))

    qkv = qkv_call(
        me,
        xa,
        xb,
        norm1[None],
        got,
        big,
        3 * hidden // width + 1,
        cos,
        sin,
        q_gain[None],
        k_gain[None],
    )
    pre_out, prefill_pages = prefill_call(
        qkv,
        pre_variate.reshape(pre_len, 1),
        pre_variate,
        pre_keep,
        bias_same,
        bias_diff,
        pre_len,
        page,
    )
    own, other = out_proj_call(
        me, bias_same, pre_out, qkv, back, pick, big, 3 * hidden // width
    )
    resid = layer_input.astype(F32) + row_scatter(own, other)
    ra, rb = row_gather(resid.astype(BF), chips)
    own, other = ffn_call(me, ra, rb, norm2[None], big, hidden)
    out = (resid + row_scatter(own, other)).astype(BF)
    tail_pages = tail_call(
        target, dec_len % page, qkv, tails.reshape(peers * slots, 2, page, width)
    )
    return (out, prefill_pages, tail_pages)


def solution(mesh):
    placed = (
        P("col", "row"),
        P("col", "row"),
        P("col", "row"),
        P("col", "row"),
        P("row", "col"),
        P("col", "row"),
        P("col", "row"),
        P("row", "col"),
        P(),
        P(),
        P("row"),
        P("row"),
        P("row"),
        P("row"),
        P("col", None),
        P("col", None),
        P("col"),
        P("col"),
        P("col", None),
        P("col", None),
        P("col", None, None, "row"),
        P("col", None),
    )
    return jax.shard_map(
        on_device,
        mesh=mesh,
        in_specs=placed,
        out_specs=(P("col", "row"), P("col", None, None, "row"), P("col", None, None, "row")),
        check_vma=False,
    )
```

```python
import functools

import jax
import jax.numpy as jnp
import numpy as np
from jax import lax
from jax.experimental import pallas as pl
from jax.experimental.pallas import tpu as pltpu
from jax.sharding import PartitionSpec as P

HD = 64
EPS = 1e-05
BF = jnp.bfloat16
F32 = jnp.float32


def dot_nt(a, b):
    return lax.dot_general(a, b, (((1,), (1,)), ((), ())), preferred_element_type=F32)


def whole(shape):
    zeros = (0,) * len(shape)
    return pl.BlockSpec(shape, lambda *_: zeros)


def in_order(me_ref, same_ref, other_ref):
    x, core = me_ref[0], me_ref[1]
    chips = same_ref.shape[0]
    parts = []
    for j in range(2 * chips):
        away = lax.rem(x - j // 2 + chips, chips)
        parts.append(jnp.where(core == j % 2, same_ref[away].astype(F32), other_ref[away].astype(F32)))
    return jnp.concatenate(parts, axis=1)


def norm_rotate(t, gain, cos, sin):
    lane = lax.broadcasted_iota(jnp.int32, t.shape, 1)
    first_head = lane < HD
    lower = (lane % HD) < (HD // 2)
    sq = t * t
    s0 = jnp.sum(jnp.where(first_head, sq, 0.0), axis=-1, keepdims=True)
    s1 = jnp.sum(jnp.where(first_head, 0.0, sq), axis=-1, keepdims=True)
    r = jnp.where(first_head, lax.rsqrt(s0 * (1.0 / HD) + EPS), lax.rsqrt(s1 * (1.0 / HD) + EPS))
    t = t * r * gain
    partner = jnp.where(
        lower, pltpu.roll(t, 128 - HD // 2, axis=1), pltpu.roll(t, HD // 2, axis=1)
    )
    return t * cos + partner * sin


def norm_features(x, gain):
    scale = lax.rsqrt(jnp.mean(x * x, axis=-1, keepdims=True) + EPS)
    return (x * scale * gain).astype(BF)


def pack_kernel(table_ref, len_ref, var_ref, holder_ref, x_ref, w_ref, *refs):
    parts, (out_ref, wide_ref) = refs[:-2], refs[-2:]
    peers = out_ref.shape[0]
    share = w_ref.shape[0]
    entries, count = table_ref.shape
    w = w_ref[...]
    for c in range(peers):
        out_ref[c, 0:share, :] = w
        out_ref[c, share : share + 8, :] = jnp.zeros((8, 128), BF)
    lane = lax.broadcasted_iota(jnp.int32, (8, 128), 1)
    sub = lax.broadcasted_iota(jnp.int32, (8, 128), 0)
    for r in range(count):
        holder = holder_ref[0, r]
        rank = jnp.int32(0)
        for p in range(r):
            rank = rank + (holder_ref[0, p] == holder).astype(jnp.int32)
        length = len_ref[r]
        facts = [table_ref[p, r] for p in range(entries)]
        facts += [length // 128, length % 128, var_ref[r]]
        vec = jnp.zeros((8, 128), jnp.int32)
        for j, fact in enumerate(facts):
            vec = jnp.where(lane == j, fact, vec)
        x = jnp.broadcast_to(x_ref[r : r + 1, :].astype(F32), (8, 128))
        old = out_ref[holder, share : share + 8, :].astype(F32)
        new = jnp.where(sub == rank, vec.astype(F32), jnp.where(sub == rank + 2, x, old))
        out_ref[holder, share : share + 8, :] = new.astype(BF)
    start = 0
    for part in parts:
        wide_ref[:, start : start + part.shape[1]] = part[...]
        start += part.shape[1]


def pack_call(table, length, variate, holder, x, w, peers, parts):
    count = length.shape[0]
    smem = pl.BlockSpec(memory_space=pltpu.SMEM)
    shape = (peers, w.shape[0] + 8, 128)
    wide = (w.shape[0], sum(p.shape[1] for p in parts))
    last = x.shape[0] // count - 1
    return pl.pallas_call(
        pack_kernel,
        grid=(1,),
        in_specs=[
            smem,
            smem,
            smem,
            smem,
            pl.BlockSpec((count, 128), lambda i: (last, 0)),
            whole(w.shape),
        ]
        + [whole(p.shape) for p in parts],
        out_specs=[whole(shape), whole(wide)],
        out_shape=[jax.ShapeDtypeStruct(shape, BF), jax.ShapeDtypeStruct(wide, BF)],
        cost_estimate=pl.CostEstimate(flops=0, bytes_accessed=1024 * 1024, transcendentals=0),
        name="pack",
    )(table, length, variate, holder, x, w, *parts)


def early_kernel(
    me_ref, xa_ref, xb_ref, norm_ref, wq_ref, cos_ref, sin_ref, qg_ref, normed_ref, q_ref
):
    normed = norm_features(in_order(me_ref, xa_ref, xb_ref), norm_ref[...])
    normed_ref[...] = normed
    wq = wq_ref[:, 0 : wq_ref.shape[1] - 8, :].reshape(-1, 128)
    q = jnp.dot(normed, wq, preferred_element_type=F32)
    q_ref[...] = norm_rotate(q, qg_ref[...], cos_ref[...], sin_ref[...]).astype(BF)


def early_call(me, xa, xb, norm1, got, cos, sin, qg):
    chips, rows, _ = xa.shape
    width = norm1.shape[1]
    step = rows // 3
    row_spec = lambda cols: pl.BlockSpec((step, cols), lambda i: (i, 0))
    x_spec = pl.BlockSpec((chips, step, 128), lambda i: (0, i, 0))
    return pl.pallas_call(
        early_kernel,
        grid=(3,),
        in_specs=[
            pl.BlockSpec(memory_space=pltpu.SMEM),
            x_spec,
            x_spec,
            whole((1, width)),
            whole(got.shape),
            row_spec(128),
            row_spec(128),
            whole((1, 128)),
        ],
        out_specs=[row_spec(width), row_spec(128)],
        out_shape=[
            jax.ShapeDtypeStruct((rows, width), BF),
            jax.ShapeDtypeStruct((rows, 128), BF),
        ],
        cost_estimate=pl.CostEstimate(
            flops=2 * rows * width * 128, bytes_accessed=4 * 1024 * 1024, transcendentals=0
        ),
        name="early",
    )(me, xa, xb, norm1, got, cos, sin, qg)


def attn_kernel(
    me_ref,
    bsame_ref,
    bdiff_ref,
    normed_ref,
    q_ref,
    wk_ref,
    wv_ref,
    wo_ref,
    cos_ref,
    sin_ref,
    kg_ref,
    vcol_ref,
    vrow_ref,
    keep_ref,
    back_ref,
    pick_ref,
    picksum_ref,
    new_ref,
    pages_ref,
    own_ref,
    other_ref,
    k_ref,
    v_ref,
):
    x, core = me_ref[0], me_ref[1]
    length = vcol_ref.shape[0]
    rows = q_ref.shape[0]
    chips = own_ref.shape[0]
    block = 128
    w = jnp.concatenate([wk_ref[...], wv_ref[...]], axis=1)
    for start in range(0, rows, block):
        end = min(start + block, rows)
        proj = jnp.dot(normed_ref[start:end, :], w, preferred_element_type=F32)
        k = norm_rotate(proj[:, 0:128], kg_ref[...], cos_ref[start:end, :], sin_ref[start:end, :])
        k_ref[start:end, :] = k.astype(BF)
        v_ref[start:end, :] = proj[:, 128:256].astype(BF)

    def put(left, start):
        size = left.shape[0]
        for away in range(chips):
            chip = lax.rem(x + away, chips)
            w_o = wo_ref[pl.ds(pl.multiple_of(chip * 256, 256), 256), :]
            o = dot_nt(left, w_o).astype(BF)
            own_ref[away, start : start + size, :] = jnp.where(core == 0, o[:, :128], o[:, 128:])
            other_ref[away, start : start + size, :] = jnp.where(core == 0, o[:, 128:], o[:, :128])

    keys = k_ref[0:length, :]
    values = v_ref[0:length, :]
    lane = lax.broadcasted_iota(jnp.int32, (block, 128), 1)
    first_head = lane < HD
    col = lax.broadcasted_iota(jnp.int32, (block, length), 1)
    row = lax.broadcasted_iota(jnp.int32, (block, length), 0)
    keep = keep_ref[...] == 1
    for b in range(length // block):
        q = q_ref[b * block : (b + 1) * block, :]
        pages_ref[b, 0] = k_ref[b * block : (b + 1) * block, :]
        pages_ref[b, 1] = v_ref[b * block : (b + 1) * block, :]
        same = vcol_ref[b * block : (b + 1) * block, :] == vrow_ref[...]
        allowed = keep | (col == row + b * block)
        outs = []
        for h in range(2):
            qh = jnp.where(first_head if h == 0 else ~first_head, q, jnp.zeros_like(q))
            s = dot_nt(qh, keys) * (HD**-0.5)
            s = s + jnp.where(same, bsame_ref[h], bdiff_ref[h])
            e = jnp.where(allowed, jnp.exp(s), 0.0)
            total = jnp.sum(e, axis=1, keepdims=True)
            weights = (e * (1.0 / total)).astype(BF)
            outs.append(jnp.dot(weights, values, preferred_element_type=F32))
        put(jnp.where(first_head, outs[0], outs[1]).astype(BF), b * block)

    kd = k_ref[length:rows, :]
    vd = v_ref[length:rows, :]
    new_ref[:, 0:128] = kd
    new_ref[:, 128:256] = vd
    first_head = first_head[0 : rows - length]
    got = jnp.dot(pick_ref[...], back_ref[...], preferred_element_type=F32)
    sums = jnp.dot(picksum_ref[...], back_ref[...], preferred_element_type=F32)
    total = jnp.where(first_head, sums[:, 0:1] + sums[:, 2:3], sums[:, 1:2] + sums[:, 3:4])
    qk = q_ref[length:rows, :].astype(F32) * kd.astype(F32)
    s0 = jnp.sum(jnp.where(first_head, qk, 0.0), axis=1, keepdims=True)
    s1 = jnp.sum(jnp.where(first_head, 0.0, qk), axis=1, keepdims=True)
    own = jnp.where(
        first_head,
        jnp.exp(s0 * (HD**-0.5) + bsame_ref[0]),
        jnp.exp(s1 * (HD**-0.5) + bsame_ref[1]),
    )
    put(((got * total + own * vd.astype(F32)) / (total + own)).astype(BF), length)


def attn_call(
    me, bsame, bdiff, normed, q, big, col_block, cos, sin, kg, vcol, vrow, keep, back, pick, picksum
):
    rows, width = normed.shape
    length = vcol.shape[0]
    chips = width // 256
    smem = pl.BlockSpec(memory_space=pltpu.SMEM)
    w_spec = lambda j: pl.BlockSpec((width, 128), lambda i: (0, col_block + j))
    half = jax.ShapeDtypeStruct((chips, rows, 128), BF)
    shapes = [
        jax.ShapeDtypeStruct((rows - length, 256), BF),
        jax.ShapeDtypeStruct((length // 128, 2, 128, 128), BF),
        half,
        half,
    ]
    tail = (cos, sin, kg, vcol, vrow, keep, back, pick, picksum)
    return pl.pallas_call(
        attn_kernel,
        grid=(1,),
        in_specs=[
            smem,
            smem,
            smem,
            whole(normed.shape),
            whole(q.shape),
            w_spec(1),
            w_spec(2),
            w_spec(0),
        ]
        + [whole(t.shape) for t in tail],
        out_specs=[whole(t.shape) for t in shapes],
        out_shape=shapes,
        scratch_shapes=[pltpu.VMEM((rows, 128), BF), pltpu.VMEM((rows, 128), BF)],
        cost_estimate=pl.CostEstimate(
            flops=8 * length * length * 128 + 6 * rows * width * 128,
            bytes_accessed=6 * 1024 * 1024,
            transcendentals=2 * length * length,
        ),
        name="attn",
    )(me, bsame, bdiff, normed, q, big, big, big, *tail)


def decode_kernel(
    me_ref,
    xa_ref,
    xb_ref,
    norm_ref,
    w_ref,
    cos_ref,
    sin_ref,
    qg_ref,
    ints_ref,
    bsame_ref,
    bdiff_ref,
    pool_ref,
    pv_ref,
    out_ref,
):
    slots = ints_ref.shape[0]
    pages = pool_ref.shape[0]
    lane = lax.broadcasted_iota(jnp.int32, (slots, 128), 1)
    first_head = lane < HD
    normed = norm_features(in_order(me_ref, xa_ref, xb_ref), norm_ref[...])
    wq = w_ref[:, 0 : w_ref.shape[1] - 8, :].reshape(-1, 128)
    q = jnp.dot(normed, wq, preferred_element_type=F32)
    q = norm_rotate(q, qg_ref[...], cos_ref[...], sin_ref[...]).astype(BF)
    zero = jnp.zeros_like(q)
    q2 = jnp.concatenate([jnp.where(first_head, q, zero), jnp.where(first_head, zero, q)], axis=0)
    rows = lax.broadcasted_iota(jnp.int32, (2 * slots, 1), 0)
    bsame = jnp.where(rows < slots, bsame_ref[0], bsame_ref[1])
    bdiff = jnp.where(rows < slots, bdiff_ref[0], bdiff_ref[1])
    ints = jnp.concatenate([ints_ref[...], ints_ref[...]], axis=0)
    entries = ints.shape[1] // 2
    last = ints[:, entries : entries + 1]
    rem = ints[:, entries + 1 : entries + 2]
    var = ints[:, entries + 2 : entries + 3]
    tok = lax.broadcasted_iota(jnp.int32, (2 * slots, 128), 1)
    in_part = (tok < rem).astype(F32)
    full = jnp.zeros((2 * slots, 128), F32)
    part = jnp.zeros((2 * slots, 128), F32)
    for p in range(entries):
        hit = (ints[:, p : p + 1] == tok).astype(F32)
        full = full + jnp.where(p < last, hit, 0.0)
        part = part + jnp.where(p == last, hit, 0.0)
    acc = jnp.zeros((2 * slots, 128), F32)
    sums = jnp.zeros((2 * slots, 128), F32)
    for g in range(pages):
        s = dot_nt(q2, pool_ref[g, 0]) * (HD**-0.5)
        s = s + jnp.where(pv_ref[g : g + 1, :] == var, bsame, bdiff)
        count = full[:, g : g + 1] + part[:, g : g + 1] * in_part
        e = jnp.exp(s) * count
        sums = sums + e
        acc = acc + jnp.dot(e.astype(BF), pool_ref[g, 1], preferred_element_type=F32)
    total = jnp.sum(sums, axis=1, keepdims=True)
    o = acc / jnp.where(total > 0.0, total, 1.0)
    o = jnp.where(first_head, o[0:slots], o[slots:]).astype(BF)
    high = total.astype(BF).astype(F32)
    low = total - high
    sums = jnp.where(
        lane < 2,
        jnp.where(lane == 0, high[0:slots], high[slots:]),
        jnp.where(lane == 2, low[0:slots], low[slots:]),
    ).astype(BF)
    peers = out_ref.shape[0]
    each = slots // peers
    at = lax.broadcasted_iota(jnp.int32, (8 * peers, slots), 0)
    slot = lax.broadcasted_iota(jnp.int32, (8 * peers, slots), 1)
    inner = at % 8
    slot = slot - (at // 8) * each
    put_o = ((inner == slot) & (slot >= 0) & (slot < each)).astype(BF)
    put_sums = ((inner == slot + each) & (slot >= 0) & (slot < each)).astype(BF)
    rows = jnp.dot(put_o, o, preferred_element_type=F32)
    rows = rows + jnp.dot(put_sums, sums, preferred_element_type=F32)
    out_ref[...] = rows.reshape(peers, 8, 128).astype(BF)


def decode_call(me, xa, xb, norm1, got, cos, sin, qg, ints, bsame, bdiff, pool, pv):
    peers = got.shape[0]
    smem = pl.BlockSpec(memory_space=pltpu.SMEM)
    args = (me, xa, xb, norm1, got, cos, sin, qg, ints, bsame, bdiff, pool, pv)
    return pl.pallas_call(
        decode_kernel,
        grid=(1,),
        in_specs=[smem if i in (0, 9, 10) else whole(a.shape) for i, a in enumerate(args)],
        out_specs=whole((peers, 8, 128)),
        out_shape=jax.ShapeDtypeStruct((peers, 8, 128), BF),
        cost_estimate=pl.CostEstimate(
            flops=4 * 128 * 128 * 4096, bytes_accessed=3 * 1024 * 1024, transcendentals=128 * 4096
        ),
        name="decode",
    )(*args)


def ffn_kernel(me_ref, ra_ref, rb_ref, norm_ref, gate_ref, up_ref, down_ref, own_ref, other_ref):
    x, core = me_ref[0], me_ref[1]
    chips = ra_ref.shape[0]
    r = in_order(me_ref, ra_ref, rb_ref)
    scale = lax.rsqrt(jnp.mean(r * r, axis=-1, keepdims=True) + EPS)
    normed = (r * scale * norm_ref[...]).astype(BF)
    gate = jnp.dot(normed, gate_ref[...], preferred_element_type=F32)
    up = jnp.dot(normed, up_ref[...], preferred_element_type=F32)
    units = (gate * (1.0 / (1.0 + jnp.exp(-gate))) * up).astype(BF)
    for away in range(chips):
        chip = lax.rem(x + away, chips)
        w = down_ref[pl.ds(pl.multiple_of(chip * 256, 256), 256), :]
        o = dot_nt(units, w).astype(BF)
        own_ref[away] = jnp.where(core == 0, o[:, :128], o[:, 128:])
        other_ref[away] = jnp.where(core == 0, o[:, 128:], o[:, :128])


def ffn_call(me, ra, rb, norm2, big, hidden):
    chips, rows, _ = ra.shape
    width = big.shape[0]
    step = rows // 3
    w_spec = lambda b: pl.BlockSpec((width, hidden), lambda i: (0, b))
    r_spec = pl.BlockSpec((chips, step, 128), lambda i: (0, i, 0))
    half = jax.ShapeDtypeStruct((chips, rows, 128), BF)
    return pl.pallas_call(
        ffn_kernel,
        grid=(3,),
        in_specs=[
            pl.BlockSpec(memory_space=pltpu.SMEM),
            r_spec,
            r_spec,
            whole((1, width)),
            w_spec(0),
            w_spec(1),
            w_spec(2),
        ],
        out_specs=[r_spec, r_spec],
        out_shape=[half, half],
        cost_estimate=pl.CostEstimate(
            flops=6 * rows * width * hidden, bytes_accessed=6 * 1024 * 1024, transcendentals=0
        ),
        compiler_params=pltpu.CompilerParams(vmem_limit_bytes=32 * 1024 * 1024),
        name="ffn",
    )(me, ra, rb, norm2, big, big, big)


def tail_kernel(target_ref, row_ref, new_ref, pages_ref, out_ref, buf, in_sem, out_sem):
    count = buf.shape[0]
    reads = [
        pltpu.make_async_copy(pages_ref.at[target_ref[r]], buf.at[r], in_sem.at[r])
        for r in range(count)
    ]
    writes = [
        pltpu.make_async_copy(buf.at[r], out_ref.at[r], out_sem.at[r]) for r in range(count)
    ]
    for c in reads:
        c.start()
    for r in range(count):
        reads[r].wait()
        row = row_ref[r]
        start = pl.multiple_of((row // 16) * 16, 16)
        hit = lax.broadcasted_iota(jnp.int32, (16, 128), 0) == row - start
        for i in range(2):
            new = new_ref[r : r + 1, i * 128 : (i + 1) * 128].astype(F32)
            old = buf[r, i, pl.ds(start, 16), :].astype(F32)
            buf[r, i, pl.ds(start, 16), :] = jnp.where(hit, new, old).astype(BF)
        writes[r].start()
    for c in writes:
        c.wait()


def tail_call(target, row, new, pages):
    count = target.shape[0]
    smem = pl.BlockSpec(memory_space=pltpu.SMEM)
    shape = (count,) + pages.shape[1:]
    return pl.pallas_call(
        tail_kernel,
        grid=(1,),
        in_specs=[
            smem,
            smem,
            whole(new.shape),
            pl.BlockSpec(memory_space=pl.ANY),
        ],
        out_specs=pl.BlockSpec(memory_space=pl.ANY),
        out_shape=jax.ShapeDtypeStruct(shape, BF),
        scratch_shapes=[
            pltpu.VMEM(shape, BF),
            pltpu.SemaphoreType.DMA((count,)),
            pltpu.SemaphoreType.DMA((count,)),
        ],
        cost_estimate=pl.CostEstimate(
            flops=0, bytes_accessed=4 * 1024 * 1024, transcendentals=0
        ),
        name="tail",
    )(target, row, new, pages)


def shifted(x, axis, size, stride, step):
    n = lax.axis_size(axis)
    span = size * stride
    pairs = []
    for i in range(n):
        place = (i % span) // stride
        pairs.append((i, i + ((place + step) % size - place) * stride))
    return lax.ppermute(x, axis, pairs)


def row_gather(v, chips):
    parts = [v] + [shifted(v, "row", chips, 2, d) for d in range(1, chips)]
    same = jnp.stack(parts)
    return same, shifted(same, "row", 2, 1, 1)


def row_scatter(own, other):
    chips = own.shape[0]
    total = own.astype(F32) + shifted(other, "row", 2, 1, 1).astype(F32)
    result = total[0]
    for d in range(1, chips):
        result = result + shifted(total[d].astype(BF), "row", chips, 2, d).astype(F32)
    return result


def exchange(x, axis):
    return lax.all_to_all(x, axis, split_axis=0, concat_axis=0, tiled=True)


def on_device(
    layer_input,
    w_q,
    w_k,
    w_v,
    w_o,
    w_gate,
    w_up,
    w_down,
    norm1,
    norm2,
    q_gain,
    k_gain,
    bias_same,
    bias_diff,
    pre_variate,
    pre_keep,
    dec_variate,
    dec_len,
    dec_table,
    dec_holder,
    kv_pool,
    page_variates,
):
    rows, width = layer_input.shape
    pre_len = pre_variate.shape[1]
    dec_count = dec_len.shape[0]
    hidden = w_gate.shape[1]
    page = kv_pool.shape[2]
    page_count = dec_table.shape[1]
    pool_pages = kv_pool.shape[0]
    peers = lax.axis_size("col")
    slots = 2
    chips = lax.axis_size("row") // 2
    row_at = lax.axis_index("row")
    me = jnp.stack([row_at // 2, row_at % 2]).astype(jnp.int32)

    sent, wide = pack_call(
        dec_table.T,
        dec_len,
        dec_variate,
        dec_holder.T,
        layer_input,
        w_q,
        peers,
        (w_gate, w_up, w_down.T, w_o.T, w_k, w_v),
    )
    got = exchange(sent, "col")
    big = lax.all_gather(wide, "col", axis=0, tiled=True)
    xa, xb = row_gather(layer_input, chips)

    slot_rows = got[:, -8 : 2 * slots - 8]
    got_x = slot_rows[:, slots:].reshape(peers * slots, width)
    sa, sb = row_gather(got_x, chips)
    got_ints = slot_rows[:, :slots, : 2 * page_count].astype(jnp.int32)
    got_ints = got_ints.reshape(peers * slots, 2 * page_count)
    got_last = got_ints[:, page_count]
    entry = jnp.arange(page_count)[None, :]
    tail_slot = jnp.sum(
        jnp.where(entry == got_last[:, None], got_ints[:, :page_count], 0), axis=1
    )
    old_tails = kv_pool[tail_slot].reshape(peers, slots, 2, page, width)

    half = HD // 2
    spacing = (jnp.arange(width) % half).astype(F32) * (2.0 / HD)
    rates = jnp.power(10000.0, -spacing)[None, :]
    sign = jnp.where((jnp.arange(width) % HD) < half, -1.0, 1.0)[None, :]

    def turns(times):
        angles = times.astype(F32)[:, None] * rates
        return jnp.cos(angles), jnp.sin(angles) * sign

    cos_slots, sin_slots = turns(got_last * page + got_ints[:, page_count + 1])
    dec = decode_call(
        me,
        sa,
        sb,
        norm1[None],
        got,
        cos_slots,
        sin_slots,
        q_gain[None],
        got_ints,
        bias_same,
        bias_diff,
        kv_pool,
        page_variates,
    )
    back = exchange(dec, "col").reshape(peers * 8, width)

    holder = dec_holder[:, 0]
    earlier = jnp.arange(dec_count)[:, None] > jnp.arange(dec_count)[None, :]
    rank = jnp.sum(((holder[:, None] == holder[None, :]) & earlier).astype(jnp.int32), axis=1)
    target = holder * slots + rank
    places = jnp.arange(peers * 8)[None, :]
    pick = (places == (holder * 8 + rank)[:, None]).astype(BF)
    picksum = (places == (holder * 8 + rank + slots)[:, None]).astype(BF)
    variates = pre_variate[0]
    starts = jnp.sum((variates[None, :] < variates[:, None]).astype(jnp.int32), axis=1)
    cos, sin = turns(jnp.concatenate([jnp.arange(pre_len) - starts, dec_len]))

    old_tails, back, cos, sin = lax.optimization_barrier((old_tails, back, cos, sin))
    tails = exchange(old_tails, "col")
    normed, q = early_call(me, xa, xb, norm1[None], got, cos, sin, q_gain[None])
    new, prefill_pages, own, other = attn_call(
        me,
        bias_same,
        bias_diff,
        normed,
        q,
        big,
        3 * hidden // width,
        cos,
        sin,
        k_gain[None],
        pre_variate.reshape(pre_len, 1),
        pre_variate,
        pre_keep,
        back,
        pick,
        picksum,
    )
    resid = layer_input.astype(F32) + row_scatter(own, other)
    ra, rb = row_gather(resid.astype(BF), chips)
    own, other = ffn_call(me, ra, rb, norm2[None], big, hidden)
    out = (resid + row_scatter(own, other)).astype(BF)
    tail_pages = tail_call(
        target, dec_len % page, new, tails.reshape(peers * slots, 2, page, width)
    )
    return (out, prefill_pages, tail_pages)


def solution(mesh):
    placed = (
        P("col", "row"),
        P("col", "row"),
        P("col", "row"),
        P("col", "row"),
        P("row", "col"),
        P("col", "row"),
        P("col", "row"),
        P("row", "col"),
        P(),
        P(),
        P("row"),
        P("row"),
        P("row"),
        P("row"),
        P("col", None),
        P("col", None),
        P("col"),
        P("col"),
        P("col", None),
        P("col", None),
        P("col", None, None, "row"),
        P("col", None),
    )
    return jax.shard_map(
        on_device,
        mesh=mesh,
        in_specs=placed,
        out_specs=(P("col", "row"), P("col", None, None, "row"), P("col", None, None, "row")),
        check_vma=False,
    )
```

```python
import functools

import jax
import jax.numpy as jnp
import numpy as np
from jax import lax
from jax.experimental import pallas as pl
from jax.experimental.pallas import tpu as pltpu
from jax.sharding import PartitionSpec as P

HD = 64
EPS = 1e-05
BF = jnp.bfloat16
F32 = jnp.float32


def dot_nt(a, b):
    return lax.dot_general(a, b, (((1,), (1,)), ((), ())), preferred_element_type=F32)


def whole(shape):
    zeros = (0,) * len(shape)
    return pl.BlockSpec(shape, lambda *_: zeros)


def in_order(me_ref, same_ref, other_ref):
    x, core = me_ref[0], me_ref[1]
    chips = same_ref.shape[0]
    parts = []
    for j in range(2 * chips):
        away = lax.rem(x - j // 2 + chips, chips)
        parts.append(jnp.where(core == j % 2, same_ref[away].astype(F32), other_ref[away].astype(F32)))
    return jnp.concatenate(parts, axis=1)


def norm_rotate(t, gain, cos, sin):
    lane = lax.broadcasted_iota(jnp.int32, t.shape, 1)
    first_head = lane < HD
    lower = (lane % HD) < (HD // 2)
    sq = t * t
    s0 = jnp.sum(jnp.where(first_head, sq, 0.0), axis=-1, keepdims=True)
    s1 = jnp.sum(jnp.where(first_head, 0.0, sq), axis=-1, keepdims=True)
    r = jnp.where(first_head, lax.rsqrt(s0 * (1.0 / HD) + EPS), lax.rsqrt(s1 * (1.0 / HD) + EPS))
    t = t * r * gain
    partner = jnp.where(
        lower, pltpu.roll(t, 128 - HD // 2, axis=1), pltpu.roll(t, HD // 2, axis=1)
    )
    return t * cos + partner * sin


def norm_features(x, gain):
    scale = lax.rsqrt(jnp.mean(x * x, axis=-1, keepdims=True) + EPS)
    return (x * scale * gain).astype(BF)


def pack_kernel(table_ref, len_ref, var_ref, holder_ref, x_ref, w_ref, *refs):
    parts, (out_ref, wide_ref) = refs[:-2], refs[-2:]
    peers = out_ref.shape[0]
    share = w_ref.shape[0]
    entries, count = table_ref.shape
    w = w_ref[...]
    for c in range(peers):
        out_ref[c, 0:share, :] = w
        out_ref[c, share : share + 8, :] = jnp.zeros((8, 128), BF)
    lane = lax.broadcasted_iota(jnp.int32, (8, 128), 1)
    sub = lax.broadcasted_iota(jnp.int32, (8, 128), 0)
    for r in range(count):
        holder = holder_ref[0, r]
        rank = jnp.int32(0)
        for p in range(r):
            rank = rank + (holder_ref[0, p] == holder).astype(jnp.int32)
        length = len_ref[r]
        facts = [table_ref[p, r] for p in range(entries)]
        facts += [length // 128, length % 128, var_ref[r]]
        vec = jnp.zeros((8, 128), jnp.int32)
        for j, fact in enumerate(facts):
            vec = jnp.where(lane == j, fact, vec)
        x = jnp.broadcast_to(x_ref[r : r + 1, :].astype(F32), (8, 128))
        old = out_ref[holder, share : share + 8, :].astype(F32)
        new = jnp.where(sub == rank, vec.astype(F32), jnp.where(sub == rank + 2, x, old))
        out_ref[holder, share : share + 8, :] = new.astype(BF)
    start = 0
    for part in parts:
        wide_ref[:, start : start + part.shape[1]] = part[...]
        start += part.shape[1]


def pack_call(table, length, variate, holder, x, w, peers, parts):
    count = length.shape[0]
    smem = pl.BlockSpec(memory_space=pltpu.SMEM)
    shape = (peers, w.shape[0] + 8, 128)
    wide = (w.shape[0], sum(p.shape[1] for p in parts))
    last = x.shape[0] // count - 1
    return pl.pallas_call(
        pack_kernel,
        grid=(1,),
        in_specs=[
            smem,
            smem,
            smem,
            smem,
            pl.BlockSpec((count, 128), lambda i: (last, 0)),
            whole(w.shape),
        ]
        + [whole(p.shape) for p in parts],
        out_specs=[whole(shape), whole(wide)],
        out_shape=[jax.ShapeDtypeStruct(shape, BF), jax.ShapeDtypeStruct(wide, BF)],
        cost_estimate=pl.CostEstimate(flops=0, bytes_accessed=1024 * 1024, transcendentals=0),
        name="pack",
    )(table, length, variate, holder, x, w, *parts)


def early_kernel(
    me_ref, xa_ref, xb_ref, norm_ref, wq_ref, cos_ref, sin_ref, qg_ref, normed_ref, q_ref
):
    normed = norm_features(in_order(me_ref, xa_ref, xb_ref), norm_ref[...])
    normed_ref[...] = normed
    wq = wq_ref[:, 0 : wq_ref.shape[1] - 8, :].reshape(-1, 128)
    q = jnp.dot(normed, wq, preferred_element_type=F32)
    q_ref[...] = norm_rotate(q, qg_ref[...], cos_ref[...], sin_ref[...]).astype(BF)


def early_call(me, xa, xb, norm1, got, cos, sin, qg):
    chips, rows, _ = xa.shape
    width = norm1.shape[1]
    step = rows // 3
    row_spec = lambda cols: pl.BlockSpec((step, cols), lambda i: (i, 0))
    x_spec = pl.BlockSpec((chips, step, 128), lambda i: (0, i, 0))
    return pl.pallas_call(
        early_kernel,
        grid=(3,),
        in_specs=[
            pl.BlockSpec(memory_space=pltpu.SMEM),
            x_spec,
            x_spec,
            whole((1, width)),
            whole(got.shape),
            row_spec(128),
            row_spec(128),
            whole((1, 128)),
        ],
        out_specs=[row_spec(width), row_spec(128)],
        out_shape=[
            jax.ShapeDtypeStruct((rows, width), BF),
            jax.ShapeDtypeStruct((rows, 128), BF),
        ],
        cost_estimate=pl.CostEstimate(
            flops=2 * rows * width * 128, bytes_accessed=4 * 1024 * 1024, transcendentals=0
        ),
        name="early",
    )(me, xa, xb, norm1, got, cos, sin, qg)


def attn_kernel(
    me_ref,
    bsame_ref,
    bdiff_ref,
    normed_ref,
    q_ref,
    wk_ref,
    wv_ref,
    wo_ref,
    cos_ref,
    sin_ref,
    kg_ref,
    vcol_ref,
    vrow_ref,
    keep_ref,
    back_ref,
    pick_ref,
    picksum_ref,
    new_ref,
    pages_ref,
    own_ref,
    other_ref,
    k_ref,
    v_ref,
):
    x, core = me_ref[0], me_ref[1]
    length = vcol_ref.shape[0]
    rows = q_ref.shape[0]
    chips = own_ref.shape[0]
    block = 128
    w = jnp.concatenate([wk_ref[...], wv_ref[...]], axis=1)
    for start in range(0, rows, block):
        end = min(start + block, rows)
        proj = jnp.dot(normed_ref[start:end, :], w, preferred_element_type=F32)
        k = norm_rotate(proj[:, 0:128], kg_ref[...], cos_ref[start:end, :], sin_ref[start:end, :])
        k_ref[start:end, :] = k.astype(BF)
        v_ref[start:end, :] = proj[:, 128:256].astype(BF)

    def put(left, start):
        size = left.shape[0]
        for away in range(chips):
            chip = lax.rem(x + away, chips)
            w_o = wo_ref[pl.ds(pl.multiple_of(chip * 256, 256), 256), :]
            o = dot_nt(left, w_o).astype(BF)
            own_ref[away, start : start + size, :] = jnp.where(core == 0, o[:, :128], o[:, 128:])
            other_ref[away, start : start + size, :] = jnp.where(core == 0, o[:, 128:], o[:, :128])

    keys = k_ref[0:length, :]
    values = v_ref[0:length, :]
    lane = lax.broadcasted_iota(jnp.int32, (block, 128), 1)
    first_head = lane < HD
    col = lax.broadcasted_iota(jnp.int32, (block, length), 1)
    row = lax.broadcasted_iota(jnp.int32, (block, length), 0)
    keep = keep_ref[...] == 1
    for b in range(length // block):
        q = q_ref[b * block : (b + 1) * block, :]
        pages_ref[b, 0] = k_ref[b * block : (b + 1) * block, :]
        pages_ref[b, 1] = v_ref[b * block : (b + 1) * block, :]
        same = vcol_ref[b * block : (b + 1) * block, :] == vrow_ref[...]
        allowed = keep | (col == row + b * block)
        outs = []
        for h in range(2):
            qh = jnp.where(first_head if h == 0 else ~first_head, q, jnp.zeros_like(q))
            s = dot_nt(qh, keys) * (HD**-0.5)
            s = s + jnp.where(same, bsame_ref[h], bdiff_ref[h])
            e = jnp.where(allowed, jnp.exp(s), 0.0)
            total = jnp.sum(e, axis=1, keepdims=True)
            weights = (e * (1.0 / total)).astype(BF)
            outs.append(jnp.dot(weights, values, preferred_element_type=F32))
        put(jnp.where(first_head, outs[0], outs[1]).astype(BF), b * block)

    kd = k_ref[length:rows, :]
    vd = v_ref[length:rows, :]
    new_ref[:, 0:128] = kd
    new_ref[:, 128:256] = vd
    first_head = first_head[0 : rows - length]
    got = jnp.dot(pick_ref[...], back_ref[...], preferred_element_type=F32)
    sums = jnp.dot(picksum_ref[...], back_ref[...], preferred_element_type=F32)
    total = jnp.where(first_head, sums[:, 0:1] + sums[:, 2:3], sums[:, 1:2] + sums[:, 3:4])
    qk = q_ref[length:rows, :].astype(F32) * kd.astype(F32)
    s0 = jnp.sum(jnp.where(first_head, qk, 0.0), axis=1, keepdims=True)
    s1 = jnp.sum(jnp.where(first_head, 0.0, qk), axis=1, keepdims=True)
    own = jnp.where(
        first_head,
        jnp.exp(s0 * (HD**-0.5) + bsame_ref[0]),
        jnp.exp(s1 * (HD**-0.5) + bsame_ref[1]),
    )
    put(((got * total + own * vd.astype(F32)) / (total + own)).astype(BF), length)


def attn_call(
    me, bsame, bdiff, normed, q, big, col_block, cos, sin, kg, vcol, vrow, keep, back, pick, picksum
):
    rows, width = normed.shape
    length = vcol.shape[0]
    chips = width // 256
    smem = pl.BlockSpec(memory_space=pltpu.SMEM)
    w_spec = lambda j: pl.BlockSpec((width, 128), lambda i: (0, col_block + j))
    half = jax.ShapeDtypeStruct((chips, rows, 128), BF)
    shapes = [
        jax.ShapeDtypeStruct((rows - length, 256), BF),
        jax.ShapeDtypeStruct((length // 128, 2, 128, 128), BF),
        half,
        half,
    ]
    tail = (cos, sin, kg, vcol, vrow, keep, back, pick, picksum)
    return pl.pallas_call(
        attn_kernel,
        grid=(1,),
        in_specs=[
            smem,
            smem,
            smem,
            whole(normed.shape),
            whole(q.shape),
            w_spec(1),
            w_spec(2),
            w_spec(0),
        ]
        + [whole(t.shape) for t in tail],
        out_specs=[whole(t.shape) for t in shapes],
        out_shape=shapes,
        scratch_shapes=[pltpu.VMEM((rows, 128), BF), pltpu.VMEM((rows, 128), BF)],
        cost_estimate=pl.CostEstimate(
            flops=8 * length * length * 128 + 6 * rows * width * 128,
            bytes_accessed=6 * 1024 * 1024,
            transcendentals=2 * length * length,
        ),
        name="attn",
    )(me, bsame, bdiff, normed, q, big, big, big, *tail)


def decode_kernel(
    me_ref,
    xa_ref,
    xb_ref,
    norm_ref,
    w_ref,
    cos_ref,
    sin_ref,
    qg_ref,
    ints_ref,
    bsame_ref,
    bdiff_ref,
    pool_ref,
    pv_ref,
    out_ref,
):
    slots = ints_ref.shape[0]
    pages = pool_ref.shape[0]
    lane = lax.broadcasted_iota(jnp.int32, (slots, 128), 1)
    first_head = lane < HD
    normed = norm_features(in_order(me_ref, xa_ref, xb_ref), norm_ref[...])
    wq = w_ref[:, 0 : w_ref.shape[1] - 8, :].reshape(-1, 128)
    q = jnp.dot(normed, wq, preferred_element_type=F32)
    q = norm_rotate(q, qg_ref[...], cos_ref[...], sin_ref[...]).astype(BF)
    zero = jnp.zeros_like(q)
    q2 = jnp.concatenate([jnp.where(first_head, q, zero), jnp.where(first_head, zero, q)], axis=0)
    rows = lax.broadcasted_iota(jnp.int32, (2 * slots, 1), 0)
    bsame = jnp.where(rows < slots, bsame_ref[0], bsame_ref[1])
    bdiff = jnp.where(rows < slots, bdiff_ref[0], bdiff_ref[1])
    ints = jnp.concatenate([ints_ref[...], ints_ref[...]], axis=0)
    entries = ints.shape[1] // 2
    last = ints[:, entries : entries + 1]
    rem = ints[:, entries + 1 : entries + 2]
    var = ints[:, entries + 2 : entries + 3]
    tok = lax.broadcasted_iota(jnp.int32, (2 * slots, 128), 1)
    in_part = (tok < rem).astype(F32)
    full = jnp.zeros((2 * slots, 128), F32)
    part = jnp.zeros((2 * slots, 128), F32)
    for p in range(entries):
        hit = (ints[:, p : p + 1] == tok).astype(F32)
        full = full + jnp.where(p < last, hit, 0.0)
        part = part + jnp.where(p == last, hit, 0.0)
    acc = jnp.zeros((2 * slots, 128), F32)
    sums = jnp.zeros((2 * slots, 128), F32)
    for g in range(pages):
        s = dot_nt(q2, pool_ref[g, 0]) * (HD**-0.5)
        s = s + jnp.where(pv_ref[g : g + 1, :] == var, bsame, bdiff)
        count = full[:, g : g + 1] + part[:, g : g + 1] * in_part
        e = jnp.exp(s) * count
        sums = sums + e
        acc = acc + jnp.dot(e.astype(BF), pool_ref[g, 1], preferred_element_type=F32)
    total = jnp.sum(sums, axis=1, keepdims=True)
    o = acc / jnp.where(total > 0.0, total, 1.0)
    o = jnp.where(first_head, o[0:slots], o[slots:]).astype(BF)
    high = total.astype(BF).astype(F32)
    low = total - high
    sums = jnp.where(
        lane < 2,
        jnp.where(lane == 0, high[0:slots], high[slots:]),
        jnp.where(lane == 2, low[0:slots], low[slots:]),
    ).astype(BF)
    peers = out_ref.shape[0]
    each = slots // peers
    at = lax.broadcasted_iota(jnp.int32, (8 * peers, slots), 0)
    slot = lax.broadcasted_iota(jnp.int32, (8 * peers, slots), 1)
    inner = at % 8
    slot = slot - (at // 8) * each
    put_o = ((inner == slot) & (slot >= 0) & (slot < each)).astype(BF)
    put_sums = ((inner == slot + each) & (slot >= 0) & (slot < each)).astype(BF)
    rows = jnp.dot(put_o, o, preferred_element_type=F32)
    rows = rows + jnp.dot(put_sums, sums, preferred_element_type=F32)
    out_ref[...] = rows.reshape(peers, 8, 128).astype(BF)


def decode_call(me, xa, xb, norm1, got, cos, sin, qg, ints, bsame, bdiff, pool, pv):
    peers = got.shape[0]
    smem = pl.BlockSpec(memory_space=pltpu.SMEM)
    args = (me, xa, xb, norm1, got, cos, sin, qg, ints, bsame, bdiff, pool, pv)
    return pl.pallas_call(
        decode_kernel,
        grid=(1,),
        in_specs=[smem if i in (0, 9, 10) else whole(a.shape) for i, a in enumerate(args)],
        out_specs=whole((peers, 8, 128)),
        out_shape=jax.ShapeDtypeStruct((peers, 8, 128), BF),
        cost_estimate=pl.CostEstimate(
            flops=4 * 128 * 128 * 4096, bytes_accessed=3 * 1024 * 1024, transcendentals=128 * 4096
        ),
        name="decode",
    )(*args)


def ffn_kernel(me_ref, ra_ref, rb_ref, norm_ref, gate_ref, up_ref, down_ref, own_ref, other_ref):
    x, core = me_ref[0], me_ref[1]
    chips = ra_ref.shape[0]
    r = in_order(me_ref, ra_ref, rb_ref)
    scale = lax.rsqrt(jnp.mean(r * r, axis=-1, keepdims=True) + EPS)
    normed = (r * scale * norm_ref[...]).astype(BF)
    gate = jnp.dot(normed, gate_ref[...], preferred_element_type=F32)
    up = jnp.dot(normed, up_ref[...], preferred_element_type=F32)
    units = (gate * (1.0 / (1.0 + jnp.exp(-gate))) * up).astype(BF)
    for away in range(chips):
        chip = lax.rem(x + away, chips)
        w = down_ref[pl.ds(pl.multiple_of(chip * 256, 256), 256), :]
        o = dot_nt(units, w).astype(BF)
        own_ref[away] = jnp.where(core == 0, o[:, :128], o[:, 128:])
        other_ref[away] = jnp.where(core == 0, o[:, 128:], o[:, :128])


def ffn_call(me, ra, rb, norm2, big, hidden):
    chips, rows, _ = ra.shape
    width = big.shape[0]
    step = rows // 3
    w_spec = lambda b: pl.BlockSpec((width, hidden), lambda i: (0, b))
    r_spec = pl.BlockSpec((chips, step, 128), lambda i: (0, i, 0))
    half = jax.ShapeDtypeStruct((chips, rows, 128), BF)
    return pl.pallas_call(
        ffn_kernel,
        grid=(3,),
        in_specs=[
            pl.BlockSpec(memory_space=pltpu.SMEM),
            r_spec,
            r_spec,
            whole((1, width)),
            w_spec(0),
            w_spec(1),
            w_spec(2),
        ],
        out_specs=[r_spec, r_spec],
        out_shape=[half, half],
        cost_estimate=pl.CostEstimate(
            flops=6 * rows * width * hidden, bytes_accessed=6 * 1024 * 1024, transcendentals=0
        ),
        compiler_params=pltpu.CompilerParams(vmem_limit_bytes=32 * 1024 * 1024),
        name="ffn",
    )(me, ra, rb, norm2, big, big, big)


def tail_kernel(target_ref, row_ref, new_ref, pages_ref, out_ref, buf, in_sem, out_sem):
    count = buf.shape[0]
    reads = [
        pltpu.make_async_copy(pages_ref.at[target_ref[r]], buf.at[r], in_sem.at[r])
        for r in range(count)
    ]
    writes = [
        pltpu.make_async_copy(buf.at[r], out_ref.at[r], out_sem.at[r]) for r in range(count)
    ]
    for c in reads:
        c.start()
    for r in range(count):
        reads[r].wait()
        row = row_ref[r]
        start = pl.multiple_of((row // 16) * 16, 16)
        hit = lax.broadcasted_iota(jnp.int32, (16, 128), 0) == row - start
        for i in range(2):
            new = new_ref[r : r + 1, i * 128 : (i + 1) * 128].astype(F32)
            old = buf[r, i, pl.ds(start, 16), :].astype(F32)
            buf[r, i, pl.ds(start, 16), :] = jnp.where(hit, new, old).astype(BF)
        writes[r].start()
    for c in writes:
        c.wait()


def tail_call(target, row, new, pages):
    count = target.shape[0]
    smem = pl.BlockSpec(memory_space=pltpu.SMEM)
    shape = (count,) + pages.shape[1:]
    return pl.pallas_call(
        tail_kernel,
        grid=(1,),
        in_specs=[
            smem,
            smem,
            whole(new.shape),
            pl.BlockSpec(memory_space=pl.ANY),
        ],
        out_specs=pl.BlockSpec(memory_space=pl.ANY),
        out_shape=jax.ShapeDtypeStruct(shape, BF),
        scratch_shapes=[
            pltpu.VMEM(shape, BF),
            pltpu.SemaphoreType.DMA((count,)),
            pltpu.SemaphoreType.DMA((count,)),
        ],
        cost_estimate=pl.CostEstimate(
            flops=0, bytes_accessed=4 * 1024 * 1024, transcendentals=0
        ),
        name="tail",
    )(target, row, new, pages)


def shifted(x, axis, size, stride, step):
    n = lax.axis_size(axis)
    span = size * stride
    pairs = []
    for i in range(n):
        place = (i % span) // stride
        pairs.append((i, i + ((place + step) % size - place) * stride))
    return lax.ppermute(x, axis, pairs)


def row_gather(v, chips):
    parts = [v] + [shifted(v, "row", chips, 2, d) for d in range(1, chips)]
    same = jnp.stack(parts)
    return same, shifted(same, "row", 2, 1, 1)


def row_scatter(own, other):
    chips = own.shape[0]
    total = own.astype(F32) + shifted(other, "row", 2, 1, 1).astype(F32)
    result = total[0]
    for d in range(1, chips):
        result = result + shifted(total[d].astype(BF), "row", chips, 2, d).astype(F32)
    return result


def exchange(x, axis):
    return lax.all_to_all(x, axis, split_axis=0, concat_axis=0, tiled=True)


def on_device(
    layer_input,
    w_q,
    w_k,
    w_v,
    w_o,
    w_gate,
    w_up,
    w_down,
    norm1,
    norm2,
    q_gain,
    k_gain,
    bias_same,
    bias_diff,
    pre_variate,
    pre_keep,
    dec_variate,
    dec_len,
    dec_table,
    dec_holder,
    kv_pool,
    page_variates,
):
    rows, width = layer_input.shape
    pre_len = pre_variate.shape[1]
    dec_count = dec_len.shape[0]
    hidden = w_gate.shape[1]
    page = kv_pool.shape[2]
    page_count = dec_table.shape[1]
    pool_pages = kv_pool.shape[0]
    peers = lax.axis_size("col")
    slots = 2
    chips = lax.axis_size("row") // 2
    row_at = lax.axis_index("row")
    me = jnp.stack([row_at // 2, row_at % 2]).astype(jnp.int32)

    sent, wide = pack_call(
        dec_table.T,
        dec_len,
        dec_variate,
        dec_holder.T,
        layer_input,
        w_q,
        peers,
        (w_gate, w_up, w_down.T, w_o.T, w_k, w_v),
    )
    got = exchange(sent, "col")
    big = lax.all_gather(wide, "col", axis=0, tiled=True)
    xa, xb = row_gather(layer_input, chips)

    slot_rows = got[:, -8 : 2 * slots - 8]
    got_x = slot_rows[:, slots:].reshape(peers * slots, width)
    sa, sb = row_gather(got_x, chips)
    got_ints = slot_rows[:, :slots, : 2 * page_count].astype(jnp.int32)
    got_ints = got_ints.reshape(peers * slots, 2 * page_count)
    got_last = got_ints[:, page_count]
    entry = jnp.arange(page_count)[None, :]
    tail_slot = jnp.sum(
        jnp.where(entry == got_last[:, None], got_ints[:, :page_count], 0), axis=1
    )
    old_tails = kv_pool[tail_slot].reshape(peers, slots, 2, page, width)

    half = HD // 2
    spacing = (jnp.arange(width) % half).astype(F32) * (2.0 / HD)
    rates = jnp.power(10000.0, -spacing)[None, :]
    sign = jnp.where((jnp.arange(width) % HD) < half, -1.0, 1.0)[None, :]

    def turns(times):
        angles = times.astype(F32)[:, None] * rates
        return jnp.cos(angles), jnp.sin(angles) * sign

    cos_slots, sin_slots = turns(got_last * page + got_ints[:, page_count + 1])
    dec = decode_call(
        me,
        sa,
        sb,
        norm1[None],
        got,
        cos_slots,
        sin_slots,
        q_gain[None],
        got_ints,
        bias_same,
        bias_diff,
        kv_pool,
        page_variates,
    )
    back = exchange(dec, "col").reshape(peers * 8, width)

    holder = dec_holder[:, 0]
    earlier = jnp.arange(dec_count)[:, None] > jnp.arange(dec_count)[None, :]
    rank = jnp.sum(((holder[:, None] == holder[None, :]) & earlier).astype(jnp.int32), axis=1)
    target = holder * slots + rank
    places = jnp.arange(peers * 8)[None, :]
    pick = (places == (holder * 8 + rank)[:, None]).astype(BF)
    picksum = (places == (holder * 8 + rank + slots)[:, None]).astype(BF)
    variates = pre_variate[0]
    starts = jnp.sum((variates[None, :] < variates[:, None]).astype(jnp.int32), axis=1)
    cos, sin = turns(jnp.concatenate([jnp.arange(pre_len) - starts, dec_len]))

    old_tails, back, cos, sin = lax.optimization_barrier((old_tails, back, cos, sin))
    tails = exchange(old_tails, "col")
    normed, q = early_call(me, xa, xb, norm1[None], got, cos, sin, q_gain[None])
    new, prefill_pages, own, other = attn_call(
        me,
        bias_same,
        bias_diff,
        normed,
        q,
        big,
        3 * hidden // width,
        cos,
        sin,
        k_gain[None],
        pre_variate.reshape(pre_len, 1),
        pre_variate,
        pre_keep,
        back,
        pick,
        picksum,
    )
    resid = layer_input.astype(F32) + row_scatter(own, other)
    ra, rb = row_gather(resid.astype(BF), chips)
    own, other = ffn_call(me, ra, rb, norm2[None], big, hidden)
    out = (resid + row_scatter(own, other)).astype(BF)
    out, tails, target, tail_row = lax.optimization_barrier(
        (out, tails, target, dec_len % page)
    )
    tail_pages = tail_call(
        target, tail_row, new, tails.reshape(peers * slots, 2, page, width)
    )
    return (out, prefill_pages, tail_pages)


def solution(mesh):
    placed = (
        P("col", "row"),
        P("col", "row"),
        P("col", "row"),
        P("col", "row"),
        P("row", "col"),
        P("col", "row"),
        P("col", "row"),
        P("row", "col"),
        P(),
        P(),
        P("row"),
        P("row"),
        P("row"),
        P("row"),
        P("col", None),
        P("col", None),
        P("col"),
        P("col"),
        P("col", None),
        P("col", None),
        P("col", None, None, "row"),
        P("col", None),
    )
    return jax.shard_map(
        on_device,
        mesh=mesh,
        in_specs=placed,
        out_specs=(P("col", "row"), P("col", None, None, "row"), P("col", None, None, "row")),
        check_vma=False,
    )
```
